32 devices in a mesh: dp: 4 (over z), tensor: 4 (over y, x), pipe: 2 (over core).
Axes of the slice: x: 2, y: 2, z: 4, core: 2. Of those that a mesh axis runs over, the one named last changes fastest.
Arguments:
- patches: bfloat16 [1280, 3072], P('tensor', ('dp', 'pipe')), may hold values from -6 to 6
- lengths: int32 [384], P(('dp', 'pipe')), may hold values from 1 to 8
- slot_plan: int32 [384], P(('dp', 'pipe')), may hold values from 0 to 47, as said below
- starts: int32 [384], P(('dp', 'pipe')), may hold values from 0 to 564, as said below
- text_rows: bfloat16 [1280, 4608], P('tensor', ('dp', 'pipe')), may hold values from -6 to 6
- cotangent: bfloat16 [1280, 4608], P('tensor', ('dp', 'pipe')), may hold values from -6 to 6
- ln_gain: float32 [1280], replicated, may hold values from 0.25 to 1.75
- ln_bias: float32 [1280], replicated, may hold values from -3 to 3
- w_qkv: bfloat16 [3, 1280, 1280], P(None, 'tensor'), may hold values from -0.15625 to 0.15625
- w_out: bfloat16 [1280, 1280], P('tensor'), may hold values from -0.15625 to 0.15625
Outputs:
- features: bfloat16 [1280, 4608], P('tensor', ('dp', 'pipe'))
- weight_grad: float32 [1280, 1280], P('tensor', ('dp', 'pipe'))
The draws below stay inside these ranges and needn't reach their ends.
Inputs may be any that keep to these rules, and one draw needn't show every extreme that they name: `slot_plan`: the 48 images of one data group have distinct slots. `starts`: within each data group the 48 places' blocks of 8 positions rise and are disjoint, separated by 0 to 4 positions, and lie inside the group's 576 positions.
All inputs are finite; a program needn't handle non-finite values.
Results may differ from the reference program's by a relative error of at most 0.0073.
Values may be sent and summed in bfloat16 or wider, within the bound.
No kernel may reach another device: no remote copies, remote signals or barrier semaphores. Data moves between devices by JAX's collectives and lax.ppermute only.
A program may use at most 64 MiB of HBM per device.

```python
import math
import jax
import jax.numpy as jnp
from jax import lax

D = 1280
HEADS = 16
HEAD_DIM = 80
LEN = 8
IMG_DEV = 48
GAP = 4
CAP = 12
SLOTS = 48
SEQ_DEV = 576
IMAGES = 384
SEQ = 4608
N_DP = 4
N_TENSOR = 4
N_PIPE = 2


def draw_slot_plan(key, part):
    group_keys = jax.random.split(jax.random.fold_in(key, 11), N_DP * N_PIPE)

    def one_group(group_key):
        return jax.random.permutation(group_key, SLOTS)[:IMG_DEV]
    return jax.vmap(one_group)(group_keys).reshape(-1).astype(jnp.int32)


def draw_starts(key, part):
    spacing = jax.random.randint(jax.random.fold_in(key, 23), (N_DP * N_PIPE, SLOTS), 0, GAP + 1)
    spacing = spacing.at[0].set(GAP)
    blocks = LEN + spacing
    ending = jnp.cumsum(blocks, axis=1)
    return (ending - blocks).reshape(-1).astype(jnp.int32)


def place_ends(drawn, key, least, largest):
    longest = drawn.shape.index(max(drawn.shape))
    spots = []
    for shift in (0, 1):
        where = [jax.random.randint(jax.random.fold_in(key, axis), (), 0, length) for axis, length in enumerate(drawn.shape)]
        where[longest] = (where[longest] + shift) % drawn.shape[longest]
        spots.append(tuple(where))
    return drawn.at[spots[0]].set(least).at[spots[1]].set(largest)


def strengthened(values, stream_key, source, target, blocks, factor):
    def block_of(axis_at):
        return (jnp.arange(values.shape[axis_at]) // (values.shape[axis_at] // blocks)).reshape((-1,) + (1,) * (values.ndim - 1 - axis_at))

    first = jax.random.permutation(stream_key, blocks)[block_of(target)]
    far = (block_of(target) + blocks // 2) % blocks
    return jnp.where((block_of(source) == first) | (block_of(source) == far), factor * values, values)


def level_of(own_key, extent, shards, smallest, top_value):
    level, own = 1.0, jax.random.fold_in(own_key, 6)
    for position, blocks in shards:
        heights = jnp.exp(jax.random.uniform(jax.random.fold_in(own, position), (blocks,), jnp.float32, smallest / len(shards), top_value / len(shards)))
        level = level * jnp.repeat(heights, extent[position] // blocks).reshape([-1 if axis == position else 1 for axis in range(len(extent))])
    return level


def noise(stream_key, shape, spread, bound, pieces=(), kind=jnp.bfloat16):
    drawn = jax.random.normal(stream_key, shape, jnp.float32) * spread
    if len(pieces) > 0:
        drawn = level_of(stream_key, shape, pieces, -0.22, 0.18) * drawn
    return jnp.clip(drawn, min=-bound, max=bound).astype(kind)


def heavy_noise(own_key, shape, deviation, bound, cuts, heavy, kind=jnp.bfloat16):
    values = deviation * jax.random.normal(own_key, shape, jnp.float32)
    if cuts:
        values = values * level_of(own_key, shape, cuts, -0.22, 0.18)
    return jnp.clip(strengthened(values, jax.random.fold_in(own_key, 3), *heavy), -bound, bound).astype(kind)


def setup_inputs(seed: int = 0) -> dict:
    splits = jax.random.split(jax.random.key(seed), 11)
    return {
        "patches": noise(splits[0], (D, IMAGES * LEN), 1.0, 6.0, ((0, 4), (1, 8))),
        "lengths": place_ends(jax.random.randint(splits[1], (IMAGES,), 1, LEN + 1), jax.random.fold_in(splits[1], 1), 1, LEN).astype(jnp.int32),
        "slot_plan": draw_slot_plan(jax.random.fold_in(splits[10], 71), 0),
        "starts": draw_starts(jax.random.fold_in(splits[10], 71), 0),
        "text_rows": noise(splits[4], (D, SEQ), 1.0, 6.0, ((0, 4), (1, 8))),
        "cotangent": heavy_noise(splits[5], (D, SEQ), 1.0, 6.0, ((0, 4), (1, 8)), (1, 0, 8, 2.0)),
        "ln_gain": jnp.clip(1.0 + 0.15 * jax.random.normal(splits[6], (D,), jnp.float32), 0.25, 1.75),
        "ln_bias": noise(splits[7], (D,), 0.5, 3.0, (), jnp.float32),
        "w_qkv": noise(splits[8], (3, D, D), D ** -0.5, 0.15625, ((1, 4),)),
        "w_out": noise(splits[9], (D, D), D ** -0.5, 0.15625, ((0, 4),)),
    }


epsilon = 1e-06

def layer_norm(inputs_f, ln_gain, ln_bias):
    average = lax.optimization_barrier(jnp.mean(inputs_f, axis=-1, keepdims=True))
    centred = inputs_f - average
    variance = lax.optimization_barrier(jnp.mean(centred * centred, axis=-1, keepdims=True))
    return centred * lax.rsqrt(variance + epsilon) * ln_gain + ln_bias

def image_block(patch_rows, lengths, ln_gain, ln_bias, w_qkv, w_out):
    count = patch_rows.shape[0]
    flat_rows = patch_rows.reshape(count * LEN, D)
    normed = layer_norm(flat_rows.astype(jnp.float32), ln_gain, ln_bias).astype(jnp.bfloat16)
    shape_heads = (count, LEN, HEADS, HEAD_DIM)
    queries = jnp.dot(normed, w_qkv[0].T, preferred_element_type=jnp.float32).astype(jnp.bfloat16).reshape(shape_heads)
    key_rows = jnp.dot(normed, w_qkv[1].T, preferred_element_type=jnp.float32).astype(jnp.bfloat16).reshape(shape_heads)
    value_rows = jnp.dot(normed, w_qkv[2].T, preferred_element_type=jnp.float32).astype(jnp.bfloat16).reshape(shape_heads)
    scores = jnp.einsum('bqhe,bkhe->bhqk', queries.astype(jnp.float32), key_rows.astype(jnp.float32))
    scores = scores * (1.0 / math.sqrt(HEAD_DIM))
    offsets = jnp.arange(LEN, dtype=jnp.int32)
    key_live = offsets[None, :] < jnp.maximum(lengths, 1)[:, None]
    scores = jnp.where(key_live[:, None, None, :], scores, -1e+30)
    top = lax.optimization_barrier(jnp.max(scores, axis=-1, keepdims=True))
    raised = jnp.exp(scores - top)
    weights = (raised / lax.optimization_barrier(jnp.sum(raised, axis=-1, keepdims=True))).astype(jnp.bfloat16)
    context = jnp.einsum('bhqk,bkhe->bqhe', weights.astype(jnp.float32), value_rows.astype(jnp.float32)).astype(jnp.bfloat16)
    is_live = offsets[None, :] < lengths[:, None]
    context = jnp.where(is_live[:, :, None, None], context, jnp.zeros_like(context))
    context = context.reshape(count * LEN, D)
    width_part = D // N_TENSOR
    attended_f = jnp.zeros((count * LEN, D), jnp.float32)
    for shard in range(N_TENSOR):
        piece = jnp.dot(context[:, shard * width_part:(shard + 1) * width_part], w_out[shard * width_part:(shard + 1) * width_part], preferred_element_type=jnp.float32)
        piece = lax.optimization_barrier(piece.astype(jnp.bfloat16))
        attended_f = attended_f + piece.astype(jnp.float32)
    attended = attended_f.astype(jnp.bfloat16)
    merged = (flat_rows.astype(jnp.float32) + attended.astype(jnp.float32)).astype(jnp.bfloat16)
    return (merged.reshape(count, LEN, D), context)

def reference(patches, lengths, slot_plan, starts, text_rows, cotangent, ln_gain, ln_bias, w_qkv, w_out):
    groups = N_DP * N_PIPE
    image_all = patches.T.reshape(groups, IMG_DEV, LEN, D)
    length_all = lengths.reshape(groups, IMG_DEV)
    slot_all = slot_plan.reshape(groups, IMG_DEV)
    offsets = jnp.arange(LEN, dtype=jnp.int32)
    cot_seq = cotangent.T

    def one_group(grad_sum, inputs):
        group_id, patch_rows, group_len, group_slot = inputs
        merged, context = image_block(patch_rows, group_len, ln_gain, ln_bias, w_qkv, w_out)
        dp_index = group_id // N_PIPE
        pipe_index = group_id % N_PIPE
        owner_index = group_slot // CAP * N_PIPE + pipe_index
        place_index = dp_index * CAP + group_slot % CAP
        block_start = starts[(owner_index * SLOTS + place_index).astype(jnp.int32)]
        row_index = owner_index[:, None] * SEQ_DEV + block_start[:, None] + offsets[None, :]
        is_live = offsets[None, :] < group_len[:, None]
        row_index = jnp.where(is_live, row_index, SEQ).astype(jnp.int32)
        cot_rows = cot_seq[jnp.minimum(row_index, SEQ - 1).reshape(-1)]
        grad_sum = grad_sum + jnp.dot(context.T, cot_rows, preferred_element_type=jnp.float32)
        return (grad_sum, (merged, row_index))
    group_ids = jnp.arange(groups, dtype=jnp.int32)
    grad_sum, (merged_all, row_all) = lax.scan(one_group, jnp.zeros((D, D), jnp.float32), (group_ids, image_all, length_all, slot_all))
    features = text_rows.T.at[row_all.reshape(-1)].set(merged_all.reshape(-1, D), mode='drop').T
    return (features, grad_sum)
```

```python
import math

import jax
import jax.numpy as jnp
from jax import lax
from jax.experimental import pallas as pl
from jax.experimental.pallas import tpu as pltpu
from jax.sharding import PartitionSpec as P

HEAD_DIM = 80


epsilon = 1e-06


def shards_any(
    patches, lengths, slot_plan, starts, text_rows, cotangent, ln_gain, ln_bias, w_qkv, w_out
):
    cols_here, flat_count = patches.shape
    image_count = lengths.shape[0]
    length = flat_count // image_count
    groups = lax.axis_size("dp")
    capacity = (image_count + groups - 1) // groups
    slot_total = groups * capacity
    heads_here = w_qkv.shape[1] // HEAD_DIM
    seq_rows = text_rows.shape[1]
    slot_ids = jnp.arange(slot_total, dtype=jnp.int32)
    picker = (slot_ids[:, None] == slot_plan[None, :]).astype(jnp.bfloat16)
    stacked = patches.reshape(cols_here, image_count, length)
    outgoing = jnp.einsum("si,cil->scl", picker, stacked, preferred_element_type=jnp.float32)
    outgoing = outgoing.astype(jnp.bfloat16).reshape(groups, capacity * cols_here * length)
    sizes_out = jnp.dot(
        picker, lengths.astype(jnp.bfloat16)[:, None], preferred_element_type=jnp.float32
    )
    sizes_out = sizes_out.astype(jnp.bfloat16).reshape(groups, capacity)
    arrived, sizes_in = (
        lax.all_to_all(outgoing, "dp", split_axis=0, concat_axis=0, tiled=True),
        lax.all_to_all(sizes_out, "dp", split_axis=0, concat_axis=0, tiled=True),
    )
    live_len = sizes_in.reshape(slot_total).astype(jnp.int32)
    own_rows = (
        arrived.reshape(slot_total, cols_here, length)
        .transpose(1, 0, 2)
        .reshape(cols_here, slot_total * length)
    )
    offsets = jnp.arange(length, dtype=jnp.int32)
    patch_pos = jnp.minimum(starts[:, None] + offsets[None, :], seq_rows - 1).reshape(-1)
    own_cot = cotangent[:, patch_pos]
    full_rows, cot_patch = (
        lax.all_gather(own_rows, "tensor", axis=0, tiled=True),
        lax.all_gather(own_cot, "tensor", axis=0, tiled=True),
    )
    inputs_f = full_rows.astype(jnp.float32)
    average = jnp.mean(inputs_f, axis=0, keepdims=True)
    centred = inputs_f - average
    variance = jnp.mean(centred * centred, axis=0, keepdims=True)
    normed = (centred * lax.rsqrt(variance + epsilon) * ln_gain[:, None] + ln_bias[:, None]).astype(
        jnp.bfloat16
    )
    shape_heads = (heads_here, HEAD_DIM, slot_total, length)
    queries = (
        jnp.dot(w_qkv[0], normed, preferred_element_type=jnp.float32)
        .astype(jnp.bfloat16)
        .reshape(shape_heads)
    )
    key_rows = (
        jnp.dot(w_qkv[1], normed, preferred_element_type=jnp.float32)
        .astype(jnp.bfloat16)
        .reshape(shape_heads)
    )
    value_rows = (
        jnp.dot(w_qkv[2], normed, preferred_element_type=jnp.float32)
        .astype(jnp.bfloat16)
        .reshape(shape_heads)
    )
    scores = jnp.einsum("hesq,hesk->hsqk", queries, key_rows, preferred_element_type=jnp.float32)
    scores = scores * (1.0 / math.sqrt(HEAD_DIM))
    key_live = offsets[None, :] < jnp.maximum(live_len, 1)[:, None]
    scores = jnp.where(key_live[None, :, None, :], scores, -1e30)
    top = jnp.max(scores, axis=-1, keepdims=True)
    raised = jnp.exp(scores - top)
    weights = (raised / jnp.sum(raised, axis=-1, keepdims=True)).astype(jnp.bfloat16)
    context = jnp.einsum(
        "hsqk,hesk->hesq", weights, value_rows, preferred_element_type=jnp.float32
    ).astype(jnp.bfloat16)
    query_live = offsets[None, :] < live_len[:, None]
    context = jnp.where(query_live[None, None, :, :], context, jnp.zeros_like(context))
    context = context.reshape(heads_here * HEAD_DIM, slot_total * length)
    head_terms = lax.dot_general(
        w_out, context, (((0,), (0,)), ((), ())), preferred_element_type=jnp.float32
    )
    attended = lax.psum_scatter(
        head_terms.astype(jnp.bfloat16), "tensor", scatter_dimension=0, tiled=True
    )
    merged = (own_rows.astype(jnp.float32) + attended.astype(jnp.float32)).astype(jnp.bfloat16)
    positions = jnp.arange(seq_rows, dtype=jnp.int32)[:, None]
    covered = (positions >= starts[None, :]) & (positions < starts[None, :] + live_len[None, :])
    source = jnp.sum(
        jnp.where(covered, slot_ids[None, :] * length + positions - starts[None, :], 0), axis=1
    )
    placed = merged[:, source]
    features = jnp.where(jnp.any(covered, axis=1)[None, :], placed, text_rows)
    grad_terms = lax.dot_general(
        context, cot_patch, (((1,), (1,)), ((), ())), preferred_element_type=jnp.float32
    )
    weight_grad = lax.psum_scatter(grad_terms, ("dp", "pipe"), scatter_dimension=1, tiled=True)
    return (features, weight_grad)


LANES = 128
NN = (((1,), (0,)), ((), ()))
NT = (((1,), (1,)), ((), ()))
TN = (((0,), (0,)), ((), ()))


def mm(left, right, dims=NN):
    return lax.dot_general(left, right, dims, preferred_element_type=jnp.float32)


def iota(shape, axis):
    return lax.broadcasted_iota(jnp.int32, shape, axis)


def onehot(condition):
    return jnp.where(condition, 1.0, 0.0).astype(jnp.bfloat16)


class Plan:
    def __init__(self, mesh, patches, lengths, text_rows, w_qkv):
        self.dp, self.tensor, self.pipe = (mesh.shape[name] for name in ("dp", "tensor", "pipe"))
        self.cols, self.flat = patches.shape
        self.images = lengths.shape[0]
        self.length = self.flat // self.images
        self.shift = self.length.bit_length() - 1
        self.capacity = (self.images + self.dp - 1) // self.dp
        self.slots = self.dp * self.capacity
        self.seq = text_rows.shape[1]
        self.width = w_qkv.shape[2]
        self.heads = w_qkv.shape[1] // HEAD_DIM
        self.block = self.capacity * self.length
        self.rest = LANES - self.block
        self.out = self.width // (self.dp * self.pipe)
        self.out_rest = self.out - LANES

    def packed(self):
        powers = all(n & (n - 1) == 0 for n in (self.dp, self.tensor, self.length))
        if not powers or self.pipe != 2 or self.dp > 8 or self.tensor > 8:
            return False
        if self.rest <= 0 or self.block % self.rest or self.images != self.slots:
            return False
        if self.flat % LANES or self.slots > 256 or self.seq > 4096 or self.width != self.cols * self.tensor:
            return False
        self.parts = self.block // self.rest
        if self.cols % ((self.parts + 1) * 16) or LANES % self.length:
            return False
        self.extra = self.cols // (self.parts + 1)
        self.main = self.extra * self.parts
        if self.out_rest <= 0 or LANES % self.out_rest or self.out_rest % 16:
            return False
        self.quarters = LANES // self.out_rest
        if self.cols % (self.quarters * 16):
            return False
        self.tail = self.cols // self.quarters
        return self.heads * HEAD_DIM == self.cols


def spread(row, picker):
    wide = jnp.broadcast_to(row.astype(jnp.float32), (8, row.shape[1])).astype(jnp.bfloat16)
    return mm(wide, picker)[0:1]


def pack_kernel(plan, slot_ref, length_ref, start_ref, patches_ref, cot_ref, *refs):
    outs, cot_out, pos_out, rows = refs[: plan.dp], refs[plan.dp], refs[plan.dp + 1], refs[plan.dp + 2]
    mine = lax.axis_index("dp")
    flat, shift, block = plan.flat, plan.shift, plan.block
    lane = iota((1, flat), 1)
    inner = lane & (plan.length - 1)
    by_image = onehot(iota((plan.images, flat), 0) == (iota((plan.images, flat), 1) >> shift))
    target = spread(slot_ref[...], by_image).astype(jnp.int32) * plan.length + inner
    rows[: plan.main] = patches_ref[: plan.main]
    size_row = spread(length_ref[...], by_image)
    rows[plan.main :] = jnp.broadcast_to(size_row, (16, flat)).astype(jnp.bfloat16)
    extra = patches_ref[plan.main :]
    at = iota((LANES, flat), 0)
    for step in range(plan.dp):
        offset = target - (mine ^ step) * block
        straight = onehot((at < block) & (at == offset))
        outs[step][...] = mm(rows[...], straight, NT).astype(jnp.bfloat16)
        for part in range(plan.parts):
            turned = onehot((at >= block) & (at - block + part * plan.rest == offset))
            here = pl.ds(part * plan.extra, plan.extra)
            both = mm(extra, turned, NT) + outs[step][here].astype(jnp.float32)
            outs[step][here] = both.astype(jnp.bfloat16)
    full_lane = iota((plan.slots, flat), 1)
    order = jnp.zeros((plan.slots, flat), jnp.int32)
    for step in range(1, plan.dp):
        order = order + jnp.where(full_lane >= step * block, 1, 0)
    place = (order ^ mine) * plan.capacity + ((full_lane - order * block) >> shift)
    by_place = onehot(iota((plan.slots, flat), 0) == place)
    starts = start_ref[...]
    high, low = spread(starts >> 4, by_place), spread(starts & 15, by_place)
    position = (high * 16.0 + low).astype(jnp.int32) + inner
    pos_out[...] = jnp.broadcast_to(position, (8, flat))
    chosen = onehot(iota((plan.seq, flat), 0) == position)
    cot_out[...] = mm(cot_ref[...], chosen).astype(jnp.bfloat16)


def unpack_kernel(plan, *refs):
    blocks, own_out, size_out, wide = refs[: plan.dp], refs[plan.dp], refs[plan.dp + 1], refs[plan.dp + 2]
    for step in range(plan.dp):
        wide[:, step * LANES : (step + 1) * LANES] = blocks[step][...]
    shape = (plan.dp * LANES, plan.flat)
    source, column = iota(shape, 0), iota(shape, 1)
    step, lane = source >> 7, source & (LANES - 1)
    goal = step * plan.block + lane
    straight = onehot((lane < plan.block) & (column == goal))
    plain = mm(wide[...], straight).astype(jnp.bfloat16)
    own_out[: plan.main] = plain[: plan.main]
    size_out[...] = plain[plan.main :]
    extra = None
    for part in range(plan.parts):
        turned = onehot((lane >= plan.block) & (column == goal - plan.block + part * plan.rest))
        term = mm(wide[part * plan.extra : (part + 1) * plan.extra], turned)
        extra = term if extra is None else extra + term
    own_out[plan.main :] = extra.astype(jnp.bfloat16)


def attend_kernel(plan, *refs):
    blocks = refs[: plan.tensor]
    size_ref, gain_ref, bias_ref, qkv_ref, out_ref = refs[plan.tensor : plan.tensor + 5]
    context_out = refs[plan.tensor + 5]
    terms_out = refs[plan.tensor + 6 : 2 * plan.tensor + 6]
    full, normed, qkv, terms = refs[2 * plan.tensor + 6 :]
    mine = lax.axis_index("tensor")
    cols = plan.cols
    for step in range(plan.tensor):
        here = pl.multiple_of((mine ^ step) * cols, 16)
        full[pl.ds(here, cols)] = blocks[step][...]
    gain = jnp.transpose(jnp.broadcast_to(gain_ref[...], (8, plan.width)))[:, 0:1]
    bias = jnp.transpose(jnp.broadcast_to(bias_ref[...], (8, plan.width)))[:, 0:1]
    rows = full[...].astype(jnp.float32)
    average = jnp.sum(rows, axis=0, keepdims=True) / plan.width
    centred = rows - average
    variance = jnp.sum(centred * centred, axis=0, keepdims=True) / plan.width
    normed[...] = (centred * lax.rsqrt(variance + epsilon) * gain + bias).astype(jnp.bfloat16)
    for kind in range(3):
        qkv[kind] = mm(qkv_ref[kind], normed[...]).astype(jnp.bfloat16)
    key_at, query_at = iota((LANES, LANES), 0), iota((LANES, LANES), 1)
    same = (key_at >> plan.shift) == (query_at >> plan.shift)
    key_inner = key_at & (plan.length - 1)
    query_inner = iota((1, LANES), 1) & (plan.length - 1)
    scale = 1.0 / math.sqrt(HEAD_DIM)
    for group in range(plan.flat // LANES):
        columns = slice(group * LANES, (group + 1) * LANES)
        size = size_ref[0:1, columns].astype(jnp.float32).astype(jnp.int32)
        live = same & (key_inner < jnp.maximum(size, 1))
        for head in range(plan.heads):
            features = slice(head * HEAD_DIM, (head + 1) * HEAD_DIM)
            scores = mm(qkv[1, features, columns], qkv[0, features, columns], TN) * scale
            scores = jnp.where(live, scores, -1e30)
            top = jnp.max(scores, axis=0, keepdims=True)
            raised = jnp.exp(scores - top)
            weights = (raised / jnp.sum(raised, axis=0, keepdims=True)).astype(jnp.bfloat16)
            context = mm(qkv[2, features, columns], weights)
            context = jnp.where(query_inner < size, context, 0.0)
            context_out[features, columns] = context.astype(jnp.bfloat16)
    terms[...] = mm(out_ref[...], context_out[...], TN).astype(jnp.bfloat16)
    for step in range(plan.tensor):
        here = pl.multiple_of((mine ^ step) * cols, 16)
        terms_out[step][...] = terms[pl.ds(here, cols)]


def place_kernel(plan, *refs):
    terms = refs[: plan.tensor]
    own_ref, size_ref, pos_ref, text_ref, features_out = refs[plan.tensor :]
    total = terms[0][...].astype(jnp.float32)
    for term in terms[1:]:
        total = total + term[...].astype(jnp.float32)
    attended = total.astype(jnp.bfloat16).astype(jnp.float32)
    merged = (own_ref[...].astype(jnp.float32) + attended).astype(jnp.bfloat16)
    inner = iota((1, plan.flat), 1) & (plan.length - 1)
    size = size_ref[0:1].astype(jnp.float32).astype(jnp.int32)
    position = jnp.where(inner < size, pos_ref[0:1], -1)
    chosen = onehot(iota((plan.seq, plan.flat), 0) == position)
    placed = mm(merged, chosen, NT).astype(jnp.bfloat16)
    covered = mm(jnp.ones((8, plan.flat), jnp.bfloat16), chosen, NT)[0:1]
    features_out[...] = jnp.where(covered > 0.5, placed, text_ref[...])


def grad_kernel(plan, context_ref, *refs):
    blocks = refs[: plan.tensor]
    keep_out, send_out, full, ordered, turned = refs[plan.tensor :]
    place, mine, core = lax.axis_index("dp"), lax.axis_index("tensor"), lax.axis_index("pipe")
    cols, rest, count = plan.cols, plan.out_rest, plan.dp * 2
    for step in range(plan.tensor):
        here = pl.multiple_of((mine ^ step) * cols, 16)
        full[pl.ds(here, cols)] = blocks[step][...]
    for index in range(count):
        step, other = index // 2, index % 2
        first = pl.multiple_of(((place ^ step) * 2 + (core ^ other)) * plan.out, 16)
        ordered[index * rest : (index + 1) * rest] = full[pl.ds(first + LANES, rest)]
        target = send_out if other else keep_out
        straight = mm(context_ref[...], full[pl.ds(first, LANES)], NT)
        target[step, :cols] = straight.astype(target.dtype)
    turned[...] = mm(context_ref[...], ordered[...], NT)
    for index in range(count):
        step, other = index // 2, index % 2
        target = send_out if other else keep_out
        for quarter in range(plan.quarters):
            piece = turned[
                quarter * plan.tail : (quarter + 1) * plan.tail, index * rest : (index + 1) * rest
            ]
            target[step, cols:, quarter * rest : (quarter + 1) * rest] = piece.astype(target.dtype)


def pair_kernel(plan, keep_ref, came_ref, own_out, *outs):
    own_out[...] = keep_ref[0] + came_ref[0].astype(jnp.float32)
    for step in range(1, plan.dp):
        total = keep_ref[step] + came_ref[step].astype(jnp.float32)
        outs[step - 1][...] = total.astype(jnp.bfloat16)


def sum_kernel(plan, own_ref, *refs):
    grad_out, total = refs[-2:]
    value = own_ref[...]
    for term in refs[:-2]:
        value = value + term[...].astype(jnp.float32)
    total[...] = value
    grad_out[:, :LANES] = total[: plan.cols]
    for quarter in range(plan.quarters):
        part = total[plan.cols :, quarter * plan.out_rest : (quarter + 1) * plan.out_rest]
        grad_out[quarter * plan.tail : (quarter + 1) * plan.tail, LANES:] = part


def call(body, plan, outs, scratch, *operands, name):
    def kernel(*refs):
        body(plan, *refs)

    return pl.pallas_call(
        kernel,
        out_shape=[jax.ShapeDtypeStruct(shape, kind) for shape, kind in outs],
        in_specs=[pl.BlockSpec(memory_space=pltpu.VMEM)] * len(operands),
        out_specs=[pl.BlockSpec(memory_space=pltpu.VMEM)] * len(outs),
        scratch_shapes=[pltpu.VMEM(shape, kind) for shape, kind in scratch],
        name=name,
    )(*operands)


def swap(value, axis, step):
    count = lax.axis_size(axis)
    return lax.ppermute(value, axis, [(index, index ^ step) for index in range(count)])


def shards_packed(
    plan, patches, lengths, slot_plan, starts, text_rows, cotangent, ln_gain, ln_bias, w_qkv, w_out
):
    half, single = jnp.bfloat16, jnp.float32
    cols, flat, width = plan.cols, plan.flat, plan.width
    height = plan.main + 16
    packed = call(
        pack_kernel, plan,
        [((height, LANES), half)] * plan.dp + [((cols, flat), half), ((8, flat), jnp.int32)],
        [((height, flat), half)],
        slot_plan[None], lengths[None], starts[None], patches, cotangent, name="pack",
    )
    blocks, own_cot, positions = packed[: plan.dp], packed[plan.dp], packed[plan.dp + 1]
    arrived = [blocks[0]] + [swap(blocks[step], "dp", step) for step in range(1, plan.dp)]
    cots = [own_cot] + [swap(own_cot, "tensor", step) for step in range(1, plan.tensor)]
    own_rows, sizes = call(
        unpack_kernel, plan,
        [((cols, flat), half), ((16, flat), half)],
        [((height, plan.dp * LANES), half)],
        *arrived, name="unpack",
    )
    rows = [own_rows] + [swap(own_rows, "tensor", step) for step in range(1, plan.tensor)]
    attended = call(
        attend_kernel, plan,
        [((cols, flat), half)] * (1 + plan.tensor),
        [((width, flat), half), ((width, flat), half), ((3, cols, flat), half), ((width, flat), half)],
        *rows, sizes, ln_gain[None], ln_bias[None], w_qkv, w_out, name="attend",
    )
    context, terms = attended[0], attended[1:]
    came = [terms[0]] + [swap(terms[step], "tensor", step) for step in range(1, plan.tensor)]
    tall = cols + plan.tail
    keep, send = call(
        grad_kernel, plan,
        [((plan.dp, tall, LANES), single), ((plan.dp, tall, LANES), half)],
        [
            ((width, flat), half),
            ((2 * plan.dp * plan.out_rest, flat), half),
            ((cols, 2 * plan.dp * plan.out_rest), single),
        ],
        context, *cots, name="grad",
    )
    pair = call(
        pair_kernel, plan,
        [((tall, LANES), single)] + [((tall, LANES), half)] * (plan.dp - 1),
        [],
        keep, swap(send, "pipe", 1), name="pair",
    )
    sums = [swap(pair[step], "dp", step) for step in range(1, plan.dp)]
    (weight_grad,) = call(
        sum_kernel, plan, [((cols, plan.out), single)], [((tall, LANES), single)],
        pair[0], *sums, name="sum",
    )
    (features,) = call(
        place_kernel, plan, [((cols, plan.seq), half)], [],
        *came, own_rows, sizes, positions, text_rows, name="place",
    )
    return (features, weight_grad)


def solution(mesh):
    placed = (
        P("tensor", ("dp", "pipe")),
        P(("dp", "pipe")),
        P(("dp", "pipe")),
        P(("dp", "pipe")),
        P("tensor", ("dp", "pipe")),
        P("tensor", ("dp", "pipe")),
        P(),
        P(),
        P(None, "tensor", None),
        P("tensor", None),
    )

    def shards(*arrays):
        plan = Plan(mesh, arrays[0], arrays[1], arrays[4], arrays[8])
        if plan.packed():
            return shards_packed(plan, *arrays)
        return shards_any(*arrays)

    return jax.shard_map(
        shards,
        mesh=mesh,
        in_specs=placed,
        out_specs=(P("tensor", ("dp", "pipe")), P("tensor", ("dp", "pipe"))),
        check_vma=False,
    )
```

```python
import math

import jax
import jax.numpy as jnp
from jax import lax
from jax.experimental import pallas as pl
from jax.experimental.pallas import tpu as pltpu
from jax.sharding import PartitionSpec as P

HEAD_DIM = 80


epsilon = 1e-06


def shards_any(
    patches, lengths, slot_plan, starts, text_rows, cotangent, ln_gain, ln_bias, w_qkv, w_out
):
    cols_here, flat_count = patches.shape
    image_count = lengths.shape[0]
    length = flat_count // image_count
    groups = lax.axis_size("dp")
    capacity = (image_count + groups - 1) // groups
    slot_total = groups * capacity
    heads_here = w_qkv.shape[1] // HEAD_DIM
    seq_rows = text_rows.shape[1]
    slot_ids = jnp.arange(slot_total, dtype=jnp.int32)
    picker = (slot_ids[:, None] == slot_plan[None, :]).astype(jnp.bfloat16)
    stacked = patches.reshape(cols_here, image_count, length)
    outgoing = jnp.einsum("si,cil->scl", picker, stacked, preferred_element_type=jnp.float32)
    outgoing = outgoing.astype(jnp.bfloat16).reshape(groups, capacity * cols_here * length)
    sizes_out = jnp.dot(
        picker, lengths.astype(jnp.bfloat16)[:, None], preferred_element_type=jnp.float32
    )
    sizes_out = sizes_out.astype(jnp.bfloat16).reshape(groups, capacity)
    arrived, sizes_in = (
        lax.all_to_all(outgoing, "dp", split_axis=0, concat_axis=0, tiled=True),
        lax.all_to_all(sizes_out, "dp", split_axis=0, concat_axis=0, tiled=True),
    )
    live_len = sizes_in.reshape(slot_total).astype(jnp.int32)
    own_rows = (
        arrived.reshape(slot_total, cols_here, length)
        .transpose(1, 0, 2)
        .reshape(cols_here, slot_total * length)
    )
    offsets = jnp.arange(length, dtype=jnp.int32)
    patch_pos = jnp.minimum(starts[:, None] + offsets[None, :], seq_rows - 1).reshape(-1)
    own_cot = cotangent[:, patch_pos]
    full_rows, cot_patch = (
        lax.all_gather(own_rows, "tensor", axis=0, tiled=True),
        lax.all_gather(own_cot, "tensor", axis=0, tiled=True),
    )
    inputs_f = full_rows.astype(jnp.float32)
    average = jnp.mean(inputs_f, axis=0, keepdims=True)
    centred = inputs_f - average
    variance = jnp.mean(centred * centred, axis=0, keepdims=True)
    normed = (centred * lax.rsqrt(variance + epsilon) * ln_gain[:, None] + ln_bias[:, None]).astype(
        jnp.bfloat16
    )
    shape_heads = (heads_here, HEAD_DIM, slot_total, length)
    queries = (
        jnp.dot(w_qkv[0], normed, preferred_element_type=jnp.float32)
        .astype(jnp.bfloat16)
        .reshape(shape_heads)
    )
    key_rows = (
        jnp.dot(w_qkv[1], normed, preferred_element_type=jnp.float32)
        .astype(jnp.bfloat16)
        .reshape(shape_heads)
    )
    value_rows = (
        jnp.dot(w_qkv[2], normed, preferred_element_type=jnp.float32)
        .astype(jnp.bfloat16)
        .reshape(shape_heads)
    )
    scores = jnp.einsum("hesq,hesk->hsqk", queries, key_rows, preferred_element_type=jnp.float32)
    scores = scores * (1.0 / math.sqrt(HEAD_DIM))
    key_live = offsets[None, :] < jnp.maximum(live_len, 1)[:, None]
    scores = jnp.where(key_live[None, :, None, :], scores, -1e30)
    top = jnp.max(scores, axis=-1, keepdims=True)
    raised = jnp.exp(scores - top)
    weights = (raised / jnp.sum(raised, axis=-1, keepdims=True)).astype(jnp.bfloat16)
    context = jnp.einsum(
        "hsqk,hesk->hesq", weights, value_rows, preferred_element_type=jnp.float32
    ).astype(jnp.bfloat16)
    query_live = offsets[None, :] < live_len[:, None]
    context = jnp.where(query_live[None, None, :, :], context, jnp.zeros_like(context))
    context = context.reshape(heads_here * HEAD_DIM, slot_total * length)
    head_terms = lax.dot_general(
        w_out, context, (((0,), (0,)), ((), ())), preferred_element_type=jnp.float32
    )
    attended = lax.psum_scatter(
        head_terms.astype(jnp.bfloat16), "tensor", scatter_dimension=0, tiled=True
    )
    merged = (own_rows.astype(jnp.float32) + attended.astype(jnp.float32)).astype(jnp.bfloat16)
    positions = jnp.arange(seq_rows, dtype=jnp.int32)[:, None]
    covered = (positions >= starts[None, :]) & (positions < starts[None, :] + live_len[None, :])
    source = jnp.sum(
        jnp.where(covered, slot_ids[None, :] * length + positions - starts[None, :], 0), axis=1
    )
    placed = merged[:, source]
    features = jnp.where(jnp.any(covered, axis=1)[None, :], placed, text_rows)
    grad_terms = lax.dot_general(
        context, cot_patch, (((1,), (1,)), ((), ())), preferred_element_type=jnp.float32
    )
    weight_grad = lax.psum_scatter(grad_terms, ("dp", "pipe"), scatter_dimension=1, tiled=True)
    return (features, weight_grad)


LANES = 128
NN = (((1,), (0,)), ((), ()))
NT = (((1,), (1,)), ((), ()))
TN = (((0,), (0,)), ((), ()))


def mm(left, right, dims=NN):
    return lax.dot_general(left, right, dims, preferred_element_type=jnp.float32)


def iota(shape, axis):
    return lax.broadcasted_iota(jnp.int32, shape, axis)


def onehot(condition):
    return jnp.where(condition, 1.0, 0.0).astype(jnp.bfloat16)


class Plan:
    def __init__(self, mesh, patches, lengths, text_rows, w_qkv):
        self.dp, self.tensor, self.pipe = (mesh.shape[name] for name in ("dp", "tensor", "pipe"))
        self.cols, self.flat = patches.shape
        self.images = lengths.shape[0]
        self.length = self.flat // self.images
        self.shift = self.length.bit_length() - 1
        self.capacity = (self.images + self.dp - 1) // self.dp
        self.slots = self.dp * self.capacity
        self.seq = text_rows.shape[1]
        self.width = w_qkv.shape[2]
        self.heads = w_qkv.shape[1] // HEAD_DIM
        self.block = self.capacity * self.length
        self.rest = LANES - self.block
        self.out = self.width // (self.dp * self.pipe)

    def packed(self):
        powers = all(n & (n - 1) == 0 for n in (self.dp, self.tensor, self.length))
        if not powers or self.pipe != 2 or self.dp > 8 or self.tensor > 8:
            return False
        if self.rest <= 0 or self.block % self.rest or self.images != self.slots:
            return False
        if self.flat % LANES or self.width % LANES or self.slots > 256 or self.seq > 4096 or self.width != self.cols * self.tensor:
            return False
        self.parts = self.block // self.rest
        if self.cols % ((self.parts + 1) * 16) or LANES % self.length:
            return False
        self.extra = self.cols // (self.parts + 1)
        self.main = self.extra * self.parts
        self.whole, last = divmod(self.cols, LANES)
        if last == 0 or LANES % last or self.out % (LANES // last * 16):
            return False
        self.pieces = LANES // last
        self.fold = self.out // self.pieces
        self.tall = self.whole * self.out + self.fold
        return self.heads * HEAD_DIM == self.cols


def spread(row, picker):
    wide = jnp.broadcast_to(row.astype(jnp.float32), (8, row.shape[1])).astype(jnp.bfloat16)
    return mm(wide, picker)[0:1]


def pack_kernel(plan, slot_ref, length_ref, start_ref, patches_ref, cot_ref, *refs):
    outs, cot_out, pos_out, rows = refs[: plan.dp], refs[plan.dp], refs[plan.dp + 1], refs[plan.dp + 2]
    mine = lax.axis_index("dp")
    flat, shift, block = plan.flat, plan.shift, plan.block
    lane = iota((1, flat), 1)
    inner = lane & (plan.length - 1)
    by_image = onehot(iota((plan.images, flat), 0) == (iota((plan.images, flat), 1) >> shift))
    target = spread(slot_ref[...], by_image).astype(jnp.int32) * plan.length + inner
    rows[: plan.main] = patches_ref[: plan.main]
    size_row = spread(length_ref[...], by_image)
    rows[plan.main :] = jnp.broadcast_to(size_row, (16, flat)).astype(jnp.bfloat16)
    extra = patches_ref[plan.main :]
    at = iota((LANES, flat), 0)
    for step in range(plan.dp):
        offset = target - (mine ^ step) * block
        straight = onehot((at < block) & (at == offset))
        outs[step][...] = mm(rows[...], straight, NT).astype(jnp.bfloat16)
        for part in range(plan.parts):
            turned = onehot((at >= block) & (at - block + part * plan.rest == offset))
            here = pl.ds(part * plan.extra, plan.extra)
            both = mm(extra, turned, NT) + outs[step][here].astype(jnp.float32)
            outs[step][here] = both.astype(jnp.bfloat16)
    full_lane = iota((plan.slots, flat), 1)
    order = jnp.zeros((plan.slots, flat), jnp.int32)
    for step in range(1, plan.dp):
        order = order + jnp.where(full_lane >= step * block, 1, 0)
    place = (order ^ mine) * plan.capacity + ((full_lane - order * block) >> shift)
    by_place = onehot(iota((plan.slots, flat), 0) == place)
    starts = start_ref[...]
    high, low = spread(starts >> 4, by_place), spread(starts & 15, by_place)
    position = (high * 16.0 + low).astype(jnp.int32) + inner
    pos_out[...] = jnp.broadcast_to(position, (8, flat))
    chosen = onehot(iota((plan.seq, flat), 0) == position)
    cot_out[...] = mm(cot_ref[...], chosen).astype(jnp.bfloat16)


def unpack_kernel(plan, *refs):
    blocks, own_out, size_out, wide = refs[: plan.dp], refs[plan.dp], refs[plan.dp + 1], refs[plan.dp + 2]
    for step in range(plan.dp):
        wide[:, step * LANES : (step + 1) * LANES] = blocks[step][...]
    shape = (plan.dp * LANES, plan.flat)
    source, column = iota(shape, 0), iota(shape, 1)
    step, lane = source >> 7, source & (LANES - 1)
    goal = step * plan.block + lane
    straight = onehot((lane < plan.block) & (column == goal))
    plain = mm(wide[...], straight).astype(jnp.bfloat16)
    own_out[: plan.main] = plain[: plan.main]
    size_out[...] = plain[plan.main :]
    extra = None
    for part in range(plan.parts):
        turned = onehot((lane >= plan.block) & (column == goal - plan.block + part * plan.rest))
        term = mm(wide[part * plan.extra : (part + 1) * plan.extra], turned)
        extra = term if extra is None else extra + term
    own_out[plan.main :] = extra.astype(jnp.bfloat16)


def prepare_kernel(plan, gain_ref, bias_ref, qkv_hbm, out_ref, qkv_out, turned_out, affine, done):
    copy = pltpu.make_async_copy(qkv_hbm, qkv_out, done)
    copy.start()
    for chunk in range(plan.width // LANES):
        here = slice(chunk * LANES, (chunk + 1) * LANES)
        for kind, vector_ref in enumerate((gain_ref, bias_ref)):
            row = jnp.broadcast_to(vector_ref[chunk : chunk + 1], (8, LANES))
            affine[kind, here] = jnp.transpose(row)
        turned_out[here] = jnp.transpose(out_ref[:, here])
    copy.wait()


def attend_kernel(plan, *refs):
    blocks = refs[: plan.tensor]
    size_ref, affine, qkv_ref, turned_ref = refs[plan.tensor : plan.tensor + 4]
    context_out = refs[plan.tensor + 4]
    terms_out = refs[plan.tensor + 5 : 2 * plan.tensor + 5]
    full, normed, qkv = refs[2 * plan.tensor + 5 :]
    mine = lax.axis_index("tensor")
    cols = plan.cols
    for step in range(plan.tensor):
        here = pl.multiple_of((mine ^ step) * cols, 16)
        full[pl.ds(here, cols)] = blocks[step][...]
    gain, bias = affine[0, :, 0:1], affine[1, :, 0:1]
    rows = full[...].astype(jnp.float32)
    average = jnp.sum(rows, axis=0, keepdims=True) / plan.width
    centred = rows - average
    variance = jnp.sum(centred * centred, axis=0, keepdims=True) / plan.width
    normed[...] = (centred * lax.rsqrt(variance + epsilon) * gain + bias).astype(jnp.bfloat16)
    for kind in range(3):
        qkv[kind] = mm(qkv_ref[kind], normed[...]).astype(jnp.bfloat16)
    key_at, query_at = iota((LANES, LANES), 0), iota((LANES, LANES), 1)
    same = (key_at >> plan.shift) == (query_at >> plan.shift)
    key_inner = key_at & (plan.length - 1)
    query_inner = iota((1, LANES), 1) & (plan.length - 1)
    scale = 1.0 / math.sqrt(HEAD_DIM)
    for group in range(plan.flat // LANES):
        columns = slice(group * LANES, (group + 1) * LANES)
        size = size_ref[0:1, columns].astype(jnp.float32).astype(jnp.int32)
        live = same & (key_inner < jnp.maximum(size, 1))
        for head in range(plan.heads):
            features = slice(head * HEAD_DIM, (head + 1) * HEAD_DIM)
            scores = mm(qkv[1, features, columns], qkv[0, features, columns], TN) * scale
            scores = jnp.where(live, scores, -1e30)
            top = jnp.max(scores, axis=0, keepdims=True)
            raised = jnp.exp(scores - top)
            weights = (raised / jnp.sum(raised, axis=0, keepdims=True)).astype(jnp.bfloat16)
            context = mm(qkv[2, features, columns], weights)
            context = jnp.where(query_inner < size, context, 0.0)
            context_out[features, columns] = context.astype(jnp.bfloat16)
    for step in range(plan.tensor):
        here = pl.multiple_of((mine ^ step) * cols, 16)
        terms_out[step][...] = mm(turned_ref[pl.ds(here, cols)], context_out[...]).astype(jnp.bfloat16)


def place_kernel(plan, *refs):
    terms = refs[: plan.tensor]
    own_ref, size_ref, pos_ref, text_ref, features_out = refs[plan.tensor :]
    total = terms[0][...].astype(jnp.float32)
    for term in terms[1:]:
        total = total + term[...].astype(jnp.float32)
    attended = total.astype(jnp.bfloat16).astype(jnp.float32)
    merged = (own_ref[...].astype(jnp.float32) + attended).astype(jnp.bfloat16)
    inner = iota((1, plan.flat), 1) & (plan.length - 1)
    size = size_ref[0:1].astype(jnp.float32).astype(jnp.int32)
    position = jnp.where(inner < size, pos_ref[0:1], -1)
    chosen = onehot(iota((plan.seq, plan.flat), 0) == position)
    placed = mm(merged, chosen, NT).astype(jnp.bfloat16)
    covered = mm(jnp.ones((8, plan.flat), jnp.bfloat16), chosen, NT)[0:1]
    features_out[...] = jnp.where(covered > 0.5, placed, text_ref[...])


def grad_kernel(plan, context_ref, *refs):
    blocks = refs[: plan.tensor]
    keep_out, send_out, full, turned = refs[plan.tensor :]
    place, mine, core = lax.axis_index("dp"), lax.axis_index("tensor"), lax.axis_index("pipe")
    cols, whole, out, fold = plan.cols, plan.whole, plan.out, plan.fold
    for step in range(plan.tensor):
        here = pl.multiple_of((mine ^ step) * cols, 16)
        full[pl.ds(here, cols)] = blocks[step][...]
    last = plan.cols - whole * LANES
    turned[...] = jnp.zeros_like(turned)
    for piece in range(plan.pieces):
        turned[piece, piece * last : (piece + 1) * last] = context_ref[whole * LANES :]
    for step in range(plan.dp):
        for other in range(2):
            target = send_out if other else keep_out
            first = pl.multiple_of(((place ^ step) * 2 + (core ^ other)) * out, 16)
            for index in range(whole):
                part = context_ref[index * LANES : (index + 1) * LANES]
                value = mm(full[pl.ds(first, out)], part, NT)
                target[step, index * out : (index + 1) * out] = value.astype(target.dtype)
            value = None
            for piece in range(plan.pieces):
                term = mm(full[pl.ds(first + piece * fold, fold)], turned[piece], NT)
                value = term if value is None else value + term
            target[step, whole * out :] = value.astype(target.dtype)


def pair_kernel(plan, keep_ref, came_ref, own_out, *outs):
    own_out[...] = keep_ref[0] + came_ref[0].astype(jnp.float32)
    for step in range(1, plan.dp):
        total = keep_ref[step] + came_ref[step].astype(jnp.float32)
        outs[step - 1][...] = total.astype(jnp.bfloat16)


def sum_kernel(plan, own_ref, *refs):
    grad_out, total = refs[-2:]
    value = own_ref[...]
    for term in refs[:-2]:
        value = value + term[...].astype(jnp.float32)
    total[...] = value
    whole, out, fold = plan.whole, plan.out, plan.fold
    last = plan.cols - whole * LANES
    for index in range(whole):
        grad_out[:, index * LANES : (index + 1) * LANES] = total[index * out : (index + 1) * out]
    for piece in range(plan.pieces):
        part = total[whole * out :, piece * last : (piece + 1) * last]
        grad_out[piece * fold : (piece + 1) * fold, whole * LANES :] = part


VMEM = pl.BlockSpec(memory_space=pltpu.VMEM)


def call(body, plan, outs, scratch, *operands, space, cost, specs=None):
    def kernel(*refs):
        body(plan, *refs)

    return pl.pallas_call(
        kernel,
        out_shape=[jax.ShapeDtypeStruct(shape, kind) for shape, kind in outs],
        in_specs=specs or [VMEM] * len(operands),
        out_specs=[VMEM] * len(outs),
        scratch_shapes=scratch,
        compiler_params=pltpu.CompilerParams(vmem_limit_bytes=space << 20),
        cost_estimate=pl.CostEstimate(flops=0, bytes_accessed=cost << 20, transcendentals=0),
    )(*operands)


def swap(value, axis, step):
    count = lax.axis_size(axis)
    return lax.ppermute(value, axis, [(index, index ^ step) for index in range(count)])


def shards_packed(
    plan, patches, lengths, slot_plan, starts, text_rows, cotangent, ln_gain, ln_bias, w_qkv, w_out
):
    half, single = jnp.bfloat16, jnp.float32
    cols, flat, width = plan.cols, plan.flat, plan.width
    height, tall = plan.main + 16, plan.tall
    packed = call(
        pack_kernel, plan,
        [((height, LANES), half)] * plan.dp + [((cols, flat), half), ((8, flat), jnp.int32)],
        [pltpu.VMEM((height, flat), half)],
        slot_plan[None], lengths[None], starts[None], patches, cotangent,
        space=8, cost=3,
    )
    blocks, own_cot, positions = packed[: plan.dp], packed[plan.dp], packed[plan.dp + 1]
    arrived = [blocks[0]] + [swap(blocks[step], "dp", step) for step in range(1, plan.dp)]
    cots = [own_cot] + [swap(own_cot, "tensor", step) for step in range(1, plan.tensor)]
    own_rows, sizes = call(
        unpack_kernel, plan,
        [((cols, flat), half), ((16, flat), half)],
        [pltpu.VMEM((height, plan.dp * LANES), half)],
        *arrived, space=6, cost=3,
    )
    rows = [own_rows] + [swap(own_rows, "tensor", step) for step in range(1, plan.tensor)]
    qkv, turned, affine = call(
        prepare_kernel, plan,
        [(w_qkv.shape, half), ((width, cols), half), ((2, width, 8), single)],
        [pltpu.SemaphoreType.DMA],
        ln_gain.reshape(-1, LANES), ln_bias.reshape(-1, LANES), w_qkv, w_out,
        space=10, cost=6,
        specs=[VMEM, VMEM, pl.BlockSpec(memory_space=pltpu.HBM), VMEM],
    )
    attended = call(
        attend_kernel, plan,
        [((cols, flat), half)] * (1 + plan.tensor),
        [
            pltpu.VMEM((width, flat), half),
            pltpu.VMEM((width, flat), half),
            pltpu.VMEM((3, cols, flat), half),
        ],
        *rows, sizes, affine, qkv, turned, space=24, cost=12,
    )
    context, terms = attended[0], attended[1:]
    came = [terms[0]] + [swap(terms[step], "tensor", step) for step in range(1, plan.tensor)]
    keep, send = call(
        grad_kernel, plan,
        [((plan.dp, tall, LANES), single), ((plan.dp, tall, LANES), half)],
        [pltpu.VMEM((width, flat), half), pltpu.VMEM((plan.pieces, LANES, flat), half)],
        context, *cots, space=10, cost=6,
    )
    pair = call(
        pair_kernel, plan,
        [((tall, LANES), single)] + [((tall, LANES), half)] * (plan.dp - 1),
        [],
        keep, swap(send, "pipe", 1), space=6, cost=3,
    )
    sums = [swap(pair[step], "dp", step) for step in range(1, plan.dp)]
    (weight_grad,) = call(
        sum_kernel, plan, [((plan.out, cols), single)], [pltpu.VMEM((tall, LANES), single)],
        pair[0], *sums, space=4, cost=2,
    )
    (features,) = call(
        place_kernel, plan, [((cols, plan.seq), half)], [],
        *came, own_rows, sizes, positions, text_rows, space=6, cost=4,
    )
    return (features, weight_grad.T)


def solution(mesh):
    placed = (
        P("tensor", ("dp", "pipe")),
        P(("dp", "pipe")),
        P(("dp", "pipe")),
        P(("dp", "pipe")),
        P("tensor", ("dp", "pipe")),
        P("tensor", ("dp", "pipe")),
        P(),
        P(),
        P(None, "tensor", None),
        P("tensor", None),
    )

    def shards(*arrays):
        plan = Plan(mesh, arrays[0], arrays[1], arrays[4], arrays[8])
        if not plan.packed():
            return shards_any(*arrays)
        return shards_packed(plan, *arrays)

    return jax.shard_map(
        shards,
        mesh=mesh,
        in_specs=placed,
        out_specs=(P("tensor", ("dp", "pipe")), P("tensor", ("dp", "pipe"))),
        check_vma=False,
    )
```

```python
import math

import jax
import jax.numpy as jnp
from jax import lax
from jax.experimental import pallas as pl
from jax.experimental.pallas import tpu as pltpu
from jax.sharding import PartitionSpec as P

HEAD_DIM = 80


epsilon = 1e-06


def shards_any(
    patches, lengths, slot_plan, starts, text_rows, cotangent, ln_gain, ln_bias, w_qkv, w_out
):
    cols_here, flat_count = patches.shape
    image_count = lengths.shape[0]
    length = flat_count // image_count
    groups = lax.axis_size("dp")
    capacity = (image_count + groups - 1) // groups
    slot_total = groups * capacity
    heads_here = w_qkv.shape[1] // HEAD_DIM
    seq_rows = text_rows.shape[1]
    slot_ids = jnp.arange(slot_total, dtype=jnp.int32)
    picker = (slot_ids[:, None] == slot_plan[None, :]).astype(jnp.bfloat16)
    stacked = patches.reshape(cols_here, image_count, length)
    outgoing = jnp.einsum("si,cil->scl", picker, stacked, preferred_element_type=jnp.float32)
    outgoing = outgoing.astype(jnp.bfloat16).reshape(groups, capacity * cols_here * length)
    sizes_out = jnp.dot(
        picker, lengths.astype(jnp.bfloat16)[:, None], preferred_element_type=jnp.float32
    )
    sizes_out = sizes_out.astype(jnp.bfloat16).reshape(groups, capacity)
    arrived, sizes_in = (
        lax.all_to_all(outgoing, "dp", split_axis=0, concat_axis=0, tiled=True),
        lax.all_to_all(sizes_out, "dp", split_axis=0, concat_axis=0, tiled=True),
    )
    live_len = sizes_in.reshape(slot_total).astype(jnp.int32)
    own_rows = (
        arrived.reshape(slot_total, cols_here, length)
        .transpose(1, 0, 2)
        .reshape(cols_here, slot_total * length)
    )
    offsets = jnp.arange(length, dtype=jnp.int32)
    patch_pos = jnp.minimum(starts[:, None] + offsets[None, :], seq_rows - 1).reshape(-1)
    own_cot = cotangent[:, patch_pos]
    full_rows, cot_patch = (
        lax.all_gather(own_rows, "tensor", axis=0, tiled=True),
        lax.all_gather(own_cot, "tensor", axis=0, tiled=True),
    )
    inputs_f = full_rows.astype(jnp.float32)
    average = jnp.mean(inputs_f, axis=0, keepdims=True)
    centred = inputs_f - average
    variance = jnp.mean(centred * centred, axis=0, keepdims=True)
    normed = (centred * lax.rsqrt(variance + epsilon) * ln_gain[:, None] + ln_bias[:, None]).astype(
        jnp.bfloat16
    )
    shape_heads = (heads_here, HEAD_DIM, slot_total, length)
    queries = (
        jnp.dot(w_qkv[0], normed, preferred_element_type=jnp.float32)
        .astype(jnp.bfloat16)
        .reshape(shape_heads)
    )
    key_rows = (
        jnp.dot(w_qkv[1], normed, preferred_element_type=jnp.float32)
        .astype(jnp.bfloat16)
        .reshape(shape_heads)
    )
    value_rows = (
        jnp.dot(w_qkv[2], normed, preferred_element_type=jnp.float32)
        .astype(jnp.bfloat16)
        .reshape(shape_heads)
    )
    scores = jnp.einsum("hesq,hesk->hsqk", queries, key_rows, preferred_element_type=jnp.float32)
    scores = scores * (1.0 / math.sqrt(HEAD_DIM))
    key_live = offsets[None, :] < jnp.maximum(live_len, 1)[:, None]
    scores = jnp.where(key_live[None, :, None, :], scores, -1e30)
    top = jnp.max(scores, axis=-1, keepdims=True)
    raised = jnp.exp(scores - top)
    weights = (raised / jnp.sum(raised, axis=-1, keepdims=True)).astype(jnp.bfloat16)
    context = jnp.einsum(
        "hsqk,hesk->hesq", weights, value_rows, preferred_element_type=jnp.float32
    ).astype(jnp.bfloat16)
    query_live = offsets[None, :] < live_len[:, None]
    context = jnp.where(query_live[None, None, :, :], context, jnp.zeros_like(context))
    context = context.reshape(heads_here * HEAD_DIM, slot_total * length)
    head_terms = lax.dot_general(
        w_out, context, (((0,), (0,)), ((), ())), preferred_element_type=jnp.float32
    )
    attended = lax.psum_scatter(
        head_terms.astype(jnp.bfloat16), "tensor", scatter_dimension=0, tiled=True
    )
    merged = (own_rows.astype(jnp.float32) + attended.astype(jnp.float32)).astype(jnp.bfloat16)
    positions = jnp.arange(seq_rows, dtype=jnp.int32)[:, None]
    covered = (positions >= starts[None, :]) & (positions < starts[None, :] + live_len[None, :])
    source = jnp.sum(
        jnp.where(covered, slot_ids[None, :] * length + positions - starts[None, :], 0), axis=1
    )
    placed = merged[:, source]
    features = jnp.where(jnp.any(covered, axis=1)[None, :], placed, text_rows)
    grad_terms = lax.dot_general(
        context, cot_patch, (((1,), (1,)), ((), ())), preferred_element_type=jnp.float32
    )
    weight_grad = lax.psum_scatter(grad_terms, ("dp", "pipe"), scatter_dimension=1, tiled=True)
    return (features, weight_grad)


LANES = 128
NN = (((1,), (0,)), ((), ()))
NT = (((1,), (1,)), ((), ()))
TN = (((0,), (0,)), ((), ()))


def mm(left, right, dims=NN):
    return lax.dot_general(left, right, dims, preferred_element_type=jnp.float32)


def iota(shape, axis):
    return lax.broadcasted_iota(jnp.int32, shape, axis)


def onehot(condition):
    return jnp.where(condition, 1.0, 0.0).astype(jnp.bfloat16)


class Plan:
    def __init__(self, mesh, patches, lengths, text_rows, w_qkv):
        self.dp, self.tensor, self.pipe = (mesh.shape[name] for name in ("dp", "tensor", "pipe"))
        self.cols, self.flat = patches.shape
        self.images = lengths.shape[0]
        self.length = self.flat // self.images
        self.shift = self.length.bit_length() - 1
        self.capacity = (self.images + self.dp - 1) // self.dp
        self.slots = self.dp * self.capacity
        self.seq = text_rows.shape[1]
        self.width = w_qkv.shape[2]
        self.heads = w_qkv.shape[1] // HEAD_DIM
        self.block = self.capacity * self.length
        self.rest = LANES - self.block
        self.out = self.width // (self.dp * self.pipe)

    def packed(self):
        powers = all(n & (n - 1) == 0 for n in (self.dp, self.tensor, self.length))
        if not powers or self.pipe != 2 or self.dp > 8 or self.tensor > 8:
            return False
        if self.rest <= 0 or self.block % self.rest or self.images != self.slots:
            return False
        if self.flat % LANES or self.width % LANES or self.slots > 256 or self.seq > 4096 or self.width != self.cols * self.tensor:
            return False
        self.parts = self.block // self.rest
        if self.cols % ((self.parts + 1) * 16) or LANES % self.length:
            return False
        self.extra = self.cols // (self.parts + 1)
        self.main = self.extra * self.parts
        self.whole, last = divmod(self.cols, LANES)
        if last == 0 or LANES % last or self.out % (LANES // last * 16):
            return False
        self.pieces = LANES // last
        self.fold = self.out // self.pieces
        self.tall = self.whole * self.out + self.fold
        return self.heads * HEAD_DIM == self.cols


def spread(row, picker):
    wide = jnp.broadcast_to(row.astype(jnp.float32), (8, row.shape[1])).astype(jnp.bfloat16)
    return mm(wide, picker)[0:1]


def pack_kernel(plan, slot_hbm, length_hbm, start_hbm, patches_hbm, cot_hbm, *refs):
    outs, cot_out, pos_out, rows = refs[: plan.dp], refs[plan.dp], refs[plan.dp + 1], refs[plan.dp + 2]
    slot_ref, length_ref, start_ref, patches_ref, cot_ref, done = refs[plan.dp + 3 :]
    held = (slot_ref, length_ref, start_ref, patches_ref, cot_ref)
    given = (slot_hbm, length_hbm, start_hbm, patches_hbm, cot_hbm)
    copies = [
        pltpu.make_async_copy(source, target, done.at[index])
        for index, (source, target) in enumerate(zip(given, held))
    ]
    for copy in copies:
        copy.start()
    for copy in copies[:4]:
        copy.wait()
    mine = lax.axis_index("dp")
    flat, shift, block = plan.flat, plan.shift, plan.block
    lane = iota((1, flat), 1)
    inner = lane & (plan.length - 1)
    by_image = onehot(iota((plan.images, flat), 0) == (iota((plan.images, flat), 1) >> shift))
    target = spread(slot_ref[...], by_image).astype(jnp.int32) * plan.length + inner
    rows[: plan.main] = patches_ref[: plan.main]
    size_row = spread(length_ref[...], by_image)
    rows[plan.main :] = jnp.broadcast_to(size_row, (16, flat)).astype(jnp.bfloat16)
    extra = patches_ref[plan.main :]
    at = iota((LANES, flat), 0)
    for step in range(plan.dp):
        offset = target - (mine ^ step) * block
        straight = onehot((at < block) & (at == offset))
        outs[step][...] = mm(rows[...], straight, NT).astype(jnp.bfloat16)
        for part in range(plan.parts):
            turned = onehot((at >= block) & (at - block + part * plan.rest == offset))
            here = pl.ds(part * plan.extra, plan.extra)
            both = mm(extra, turned, NT) + outs[step][here].astype(jnp.float32)
            outs[step][here] = both.astype(jnp.bfloat16)
    full_lane = iota((plan.slots, flat), 1)
    order = jnp.zeros((plan.slots, flat), jnp.int32)
    for step in range(1, plan.dp):
        order = order + jnp.where(full_lane >= step * block, 1, 0)
    place = (order ^ mine) * plan.capacity + ((full_lane - order * block) >> shift)
    by_place = onehot(iota((plan.slots, flat), 0) == place)
    starts = start_ref[...]
    high, low = spread(starts >> 4, by_place), spread(starts & 15, by_place)
    position = (high * 16.0 + low).astype(jnp.int32) + inner
    pos_out[...] = jnp.broadcast_to(position, (8, flat))
    chosen = onehot(iota((plan.seq, flat), 0) == position)
    copies[4].wait()
    cot_out[...] = mm(cot_ref[...], chosen).astype(jnp.bfloat16)


def unpack_kernel(plan, *refs):
    blocks, own_out, size_out, wide = refs[: plan.dp], refs[plan.dp], refs[plan.dp + 1], refs[plan.dp + 2]
    for step in range(plan.dp):
        wide[:, step * LANES : (step + 1) * LANES] = blocks[step][...]
    shape = (plan.dp * LANES, plan.flat)
    source, column = iota(shape, 0), iota(shape, 1)
    step, lane = source >> 7, source & (LANES - 1)
    goal = step * plan.block + lane
    straight = onehot((lane < plan.block) & (column == goal))
    plain = mm(wide[...], straight).astype(jnp.bfloat16)
    own_out[: plan.main] = plain[: plan.main]
    size_out[...] = plain[plan.main :]
    extra = None
    for part in range(plan.parts):
        turned = onehot((lane >= plan.block) & (column == goal - plan.block + part * plan.rest))
        term = mm(wide[part * plan.extra : (part + 1) * plan.extra], turned)
        extra = term if extra is None else extra + term
    own_out[plan.main :] = extra.astype(jnp.bfloat16)


def prepare_kernel(plan, gain_ref, bias_ref, qkv_hbm, out_ref, qkv_out, turned_out, affine, done):
    copy = pltpu.make_async_copy(qkv_hbm, qkv_out, done)
    copy.start()
    for chunk in range(plan.width // LANES):
        here = slice(chunk * LANES, (chunk + 1) * LANES)
        for kind, vector_ref in enumerate((gain_ref, bias_ref)):
            row = jnp.broadcast_to(vector_ref[chunk : chunk + 1], (8, LANES))
            affine[kind, here] = jnp.transpose(row)
        turned_out[here] = jnp.transpose(out_ref[:, here])
    copy.wait()


def attend_kernel(plan, *refs):
    blocks = refs[: plan.tensor]
    size_ref, affine, qkv_ref, turned_ref = refs[plan.tensor : plan.tensor + 4]
    context_out = refs[plan.tensor + 4]
    terms_out = refs[plan.tensor + 5 : 2 * plan.tensor + 5]
    full, normed, qkv = refs[2 * plan.tensor + 5 :]
    mine = lax.axis_index("tensor")
    cols = plan.cols
    for step in range(plan.tensor):
        here = pl.multiple_of((mine ^ step) * cols, 16)
        full[pl.ds(here, cols)] = blocks[step][...]
    gain, bias = affine[0, :, 0:1], affine[1, :, 0:1]
    rows = full[...].astype(jnp.float32)
    average = jnp.sum(rows, axis=0, keepdims=True) / plan.width
    centred = rows - average
    variance = jnp.sum(centred * centred, axis=0, keepdims=True) / plan.width
    normed[...] = (centred * lax.rsqrt(variance + epsilon) * gain + bias).astype(jnp.bfloat16)
    for kind in range(3):
        qkv[kind] = mm(qkv_ref[kind], normed[...]).astype(jnp.bfloat16)
    key_at, query_at = iota((LANES, LANES), 0), iota((LANES, LANES), 1)
    same = (key_at >> plan.shift) == (query_at >> plan.shift)
    key_inner = key_at & (plan.length - 1)
    query_inner = iota((1, LANES), 1) & (plan.length - 1)
    scale = 1.0 / math.sqrt(HEAD_DIM)
    for group in range(plan.flat // LANES):
        columns = slice(group * LANES, (group + 1) * LANES)
        size = size_ref[0:1, columns].astype(jnp.float32).astype(jnp.int32)
        live = same & (key_inner < jnp.maximum(size, 1))
        for head in range(plan.heads):
            features = slice(head * HEAD_DIM, (head + 1) * HEAD_DIM)
            scores = mm(qkv[1, features, columns], qkv[0, features, columns], TN) * scale
            scores = jnp.where(live, scores, -1e30)
            top = jnp.max(scores, axis=0, keepdims=True)
            raised = jnp.exp(scores - top)
            weights = (raised / jnp.sum(raised, axis=0, keepdims=True)).astype(jnp.bfloat16)
            context = mm(qkv[2, features, columns], weights)
            context = jnp.where(query_inner < size, context, 0.0)
            context_out[features, columns] = context.astype(jnp.bfloat16)
    for step in range(plan.tensor):
        here = pl.multiple_of((mine ^ step) * cols, 16)
        terms_out[step][...] = mm(turned_ref[pl.ds(here, cols)], context_out[...]).astype(jnp.bfloat16)


def place_kernel(plan, *refs):
    terms = refs[: plan.tensor]
    own_ref, size_ref, pos_ref, text_ref, features_out = refs[plan.tensor :]
    total = terms[0][...].astype(jnp.float32)
    for term in terms[1:]:
        total = total + term[...].astype(jnp.float32)
    attended = total.astype(jnp.bfloat16).astype(jnp.float32)
    merged = (own_ref[...].astype(jnp.float32) + attended).astype(jnp.bfloat16)
    inner = iota((1, plan.flat), 1) & (plan.length - 1)
    size = size_ref[0:1].astype(jnp.float32).astype(jnp.int32)
    position = jnp.where(inner < size, pos_ref[0:1], -1)
    chosen = onehot(iota((plan.seq, plan.flat), 0) == position)
    placed = mm(merged, chosen, NT).astype(jnp.bfloat16)
    covered = mm(jnp.ones((8, plan.flat), jnp.bfloat16), chosen, NT)[0:1]
    features_out[...] = jnp.where(covered > 0.5, placed, text_ref[...])


def grad_kernel(plan, context_ref, *refs):
    blocks = refs[: plan.tensor]
    keep_out, send_out, full, turned = refs[plan.tensor :]
    place, mine, core = lax.axis_index("dp"), lax.axis_index("tensor"), lax.axis_index("pipe")
    cols, whole, out, fold = plan.cols, plan.whole, plan.out, plan.fold
    for step in range(plan.tensor):
        here = pl.multiple_of((mine ^ step) * cols, 16)
        full[pl.ds(here, cols)] = blocks[step][...]
    last = plan.cols - whole * LANES
    turned[...] = jnp.zeros_like(turned)
    for piece in range(plan.pieces):
        turned[piece, piece * last : (piece + 1) * last] = context_ref[whole * LANES :]
    for step in range(plan.dp):
        for other in range(2):
            target = send_out if other else keep_out
            first = pl.multiple_of(((place ^ step) * 2 + (core ^ other)) * out, 16)
            for index in range(whole):
                part = context_ref[index * LANES : (index + 1) * LANES]
                value = mm(full[pl.ds(first, out)], part, NT)
                target[step, index * out : (index + 1) * out] = value.astype(target.dtype)
            value = None
            for piece in range(plan.pieces):
                term = mm(full[pl.ds(first + piece * fold, fold)], turned[piece], NT)
                value = term if value is None else value + term
            target[step, whole * out :] = value.astype(target.dtype)


def pair_kernel(plan, keep_ref, came_ref, own_out, *outs):
    own_out[...] = keep_ref[0] + came_ref[0].astype(jnp.float32)
    for step in range(1, plan.dp):
        total = keep_ref[step] + came_ref[step].astype(jnp.float32)
        outs[step - 1][...] = total.astype(jnp.bfloat16)


def sum_kernel(plan, own_ref, *refs):
    grad_out, total = refs[-2:]
    value = own_ref[...]
    for term in refs[:-2]:
        value = value + term[...].astype(jnp.float32)
    total[...] = value
    whole, out, fold = plan.whole, plan.out, plan.fold
    last = plan.cols - whole * LANES
    for index in range(whole):
        grad_out[:, index * LANES : (index + 1) * LANES] = total[index * out : (index + 1) * out]
    for piece in range(plan.pieces):
        part = total[whole * out :, piece * last : (piece + 1) * last]
        grad_out[piece * fold : (piece + 1) * fold, whole * LANES :] = part


VMEM = pl.BlockSpec(memory_space=pltpu.VMEM)
FAR = pl.BlockSpec(memory_space=pltpu.HBM)


def far(value):
    return pltpu.with_memory_space_constraint(value, pltpu.HBM)


def call(body, plan, outs, scratch, *operands, space, cost, specs=None):
    def kernel(*refs):
        body(plan, *refs)

    return pl.pallas_call(
        kernel,
        out_shape=[jax.ShapeDtypeStruct(shape, kind) for shape, kind in outs],
        in_specs=specs or [VMEM] * len(operands),
        out_specs=[VMEM] * len(outs),
        scratch_shapes=scratch,
        compiler_params=pltpu.CompilerParams(vmem_limit_bytes=space << 20),
        cost_estimate=pl.CostEstimate(flops=0, bytes_accessed=cost << 20, transcendentals=0),
    )(*operands)


def swap(value, axis, step):
    count = lax.axis_size(axis)
    return lax.ppermute(value, axis, [(index, index ^ step) for index in range(count)])


def shards_packed(
    plan, patches, lengths, slot_plan, starts, text_rows, cotangent, ln_gain, ln_bias, w_qkv, w_out
):
    half, single = jnp.bfloat16, jnp.float32
    cols, flat, width = plan.cols, plan.flat, plan.width
    height, tall = plan.main + 16, plan.tall
    packed = call(
        pack_kernel, plan,
        [((height, LANES), half)] * plan.dp + [((cols, flat), half), ((8, flat), jnp.int32)],
        [
            pltpu.VMEM((height, flat), half),
            *[pltpu.VMEM((1, count), jnp.int32) for count in (plan.images, plan.images, plan.slots)],
            pltpu.VMEM(patches.shape, half),
            pltpu.VMEM(cotangent.shape, half),
            pltpu.SemaphoreType.DMA((5,)),
        ],
        *[far(value) for value in (slot_plan[None], lengths[None], starts[None], patches, cotangent)],
        space=8, cost=3, specs=[FAR] * 5,
    )
    blocks, own_cot, positions = packed[: plan.dp], packed[plan.dp], packed[plan.dp + 1]
    arrived = [blocks[0]] + [swap(blocks[step], "dp", step) for step in range(1, plan.dp)]
    cots = [own_cot] + [swap(own_cot, "tensor", step) for step in range(1, plan.tensor)]
    own_rows, sizes = call(
        unpack_kernel, plan,
        [((cols, flat), half), ((16, flat), half)],
        [pltpu.VMEM((height, plan.dp * LANES), half)],
        *arrived, space=6, cost=3,
    )
    rows = [own_rows] + [swap(own_rows, "tensor", step) for step in range(1, plan.tensor)]
    qkv, turned, affine = call(
        prepare_kernel, plan,
        [(w_qkv.shape, half), ((width, cols), half), ((2, width, 8), single)],
        [pltpu.SemaphoreType.DMA],
        ln_gain.reshape(-1, LANES), ln_bias.reshape(-1, LANES), far(w_qkv), w_out,
        space=10, cost=6, specs=[VMEM, VMEM, FAR, VMEM],
    )
    attended = call(
        attend_kernel, plan,
        [((cols, flat), half)] * (1 + plan.tensor),
        [
            pltpu.VMEM((width, flat), half),
            pltpu.VMEM((width, flat), half),
            pltpu.VMEM((3, cols, flat), half),
        ],
        *rows, sizes, affine, qkv, turned, space=24, cost=12,
    )
    context, terms = attended[0], attended[1:]
    came = [terms[0]] + [swap(terms[step], "tensor", step) for step in range(1, plan.tensor)]
    keep, send = call(
        grad_kernel, plan,
        [((plan.dp, tall, LANES), single), ((plan.dp, tall, LANES), half)],
        [pltpu.VMEM((width, flat), half), pltpu.VMEM((plan.pieces, LANES, flat), half)],
        context, *cots, space=10, cost=6,
    )
    pair = call(
        pair_kernel, plan,
        [((tall, LANES), single)] + [((tall, LANES), half)] * (plan.dp - 1),
        [],
        keep, swap(send, "pipe", 1), space=6, cost=3,
    )
    sums = [swap(pair[step], "dp", step) for step in range(1, plan.dp)]
    (weight_grad,) = call(
        sum_kernel, plan, [((plan.out, cols), single)], [pltpu.VMEM((tall, LANES), single)],
        pair[0], *sums, space=4, cost=2,
    )
    (features,) = call(
        place_kernel, plan, [((cols, plan.seq), half)], [],
        *came, own_rows, sizes, positions, text_rows, space=6, cost=4,
    )
    return (features, weight_grad.T)


def solution(mesh):
    placed = (
        P("tensor", ("dp", "pipe")),
        P(("dp", "pipe")),
        P(("dp", "pipe")),
        P(("dp", "pipe")),
        P("tensor", ("dp", "pipe")),
        P("tensor", ("dp", "pipe")),
        P(),
        P(),
        P(None, "tensor", None),
        P("tensor", None),
    )

    def shards(*arrays):
        plan = Plan(mesh, arrays[0], arrays[1], arrays[4], arrays[8])
        if not plan.packed():
            return shards_any(*arrays)
        return shards_packed(plan, *arrays)

    return jax.shard_map(
        shards,
        mesh=mesh,
        in_specs=placed,
        out_specs=(P("tensor", ("dp", "pipe")), P("tensor", ("dp", "pipe"))),
        check_vma=False,
    )
```
